1024 devices in a mesh: member: 64 (over z, x), region: 16 (over y, core).
Axes of the slice: x: 4, y: 8, z: 16, core: 2. Of those that a mesh axis runs over, the one named last changes fastest.
Arguments:
- ensemble: bfloat16 [1024, 16, 64, 512], P('member', 'region'), may hold values from -6 to 6
- obs_store: bfloat16 [16, 64, 5, 128, 1024], P('region', 'member'), may hold values from -4 to 4
- block_ids: int32 [16, 64, 3], P('region', 'member'), may hold values from 0 to 4, as said below
- block_src: int32 [16, 64, 3], P('region', 'member'), may hold values from 0 to 2, as said below
- block_count: int32 [16, 64], P('region', 'member'), may hold values from 1 to 3, as said below
Outputs:
- analysis: bfloat16 [1024, 16, 64, 512], P('member', 'region')
The draws below stay inside these ranges and needn't reach their ends.
Inputs may be any that keep to these rules, and one draw needn't show every extreme that they name: `block_ids`: within one patch's list the first 3 entries are distinct store indices. `block_src`: region 0 never names the region below and region 16 - 1 never names the region above. `block_count`: every region has a patch with 3 blocks.
All inputs are finite; a program needn't handle non-finite values.
Results may differ from the reference program's by a relative error of at most 0.0021.
Values may be sent and summed in bfloat16 or wider, within the bound.
A program may use at most 32 MiB of HBM per device.

```python
import jax
import jax.numpy as jnp
from jax import lax

K = 1024
V = 512
ROWS = 128
OBS_DEV = 5
MAXB = 3
REGIONS = 16
PATCHES = 64


def draw_obs_store(key, part):
    shape = (REGIONS, PATCHES, OBS_DEV, ROWS, K)
    main_key = jax.random.fold_in(key, 101)
    values = 0.6 * jax.random.normal(main_key, shape, jnp.float32)
    return jnp.clip(values, -4.0, 4.0).astype(jnp.bfloat16)


def draw_block_ids(key, part):
    scores = jax.random.randint(key, (REGIONS, PATCHES, OBS_DEV), 0, 1 << 20)
    scores = scores * OBS_DEV + jnp.arange(OBS_DEV, dtype=jnp.int32)[None, None, :]
    order_ids = jnp.argsort(scores, axis=-1, stable=True)
    return order_ids[:, :, :MAXB].astype(jnp.int32)


def draw_block_src(key, part):
    codes = jax.random.randint(key, (REGIONS, PATCHES, MAXB), 0, 3)
    region_idx = jnp.arange(REGIONS, dtype=jnp.int32)[:, None, None]
    codes = jnp.where((region_idx == 0) & (codes == 0), 1, codes)
    codes = jnp.where((region_idx == REGIONS - 1) & (codes == 2), 1, codes)
    return codes.astype(jnp.int32)


def draw_block_count(key, part):
    first_key = jax.random.fold_in(key, 11)
    second_key = jax.random.fold_in(key, 23)
    counts = jax.random.randint(first_key, (REGIONS, PATCHES), 1, MAXB + 1)
    chosen = jax.random.randint(second_key, (REGIONS,), 0, PATCHES)
    patch_idx = jnp.arange(PATCHES, dtype=jnp.int32)[None, :]
    counts = jnp.where(patch_idx == chosen[:, None], MAXB, counts)
    return counts.astype(jnp.int32)


def block_scale(stream_key, shape, split, least, high):
    def one(position, parts):
        draws = jax.random.uniform(jax.random.fold_in(jax.random.fold_in(stream_key, 6), position), (parts,), jnp.float32, least / len(split), high / len(split))
        return jnp.repeat(jnp.exp(draws), shape[position] // parts).reshape((-1,) + (1,) * (len(shape) - position - 1))

    level = one(*split[0])
    for cut in split[1:]:
        level = level * one(*cut)
    return level


def scatter_about(key, extent, scale, reach, cuts=(), kind=jnp.bfloat16):
    gain = block_scale(key, extent, cuts, -0.22, 0.18) if cuts else 1.0
    values = jax.random.normal(key, extent, jnp.float32) * scale * gain
    return jnp.minimum(jnp.maximum(values, -reach), reach).astype(kind)


def setup_inputs(seed: int = 0) -> dict:
    key_list = jax.random.split(jax.random.key(seed), 6)
    return {
        "ensemble": scatter_about(key_list[0], (K, REGIONS, PATCHES, V), 1.0, 6.0, ((0, 64), (1, 16))),
        "obs_store": draw_obs_store(jax.random.fold_in(key_list[5], 71), 0),
        "block_ids": draw_block_ids(jax.random.fold_in(key_list[5], 71), 0),
        "block_src": draw_block_src(jax.random.fold_in(key_list[5], 71), 0),
        "block_count": draw_block_count(jax.random.fold_in(key_list[5], 71), 0),
    }


def reference(ensemble, obs_store, block_ids, block_src, block_count):
    regions = block_count.shape[0]
    patches = block_count.shape[1]
    highest = lax.Precision.HIGHEST

    def one_patch(index):
        region = index // patches
        patch = index % patches
        slot_ids = block_ids[region, patch]
        slot_src = block_src[region, patch]
        used = block_count[region, patch]
        source = jnp.clip(region + slot_src - 1, 0, regions - 1)
        blocks = obs_store[source, patch, slot_ids]
        live_slots = jnp.arange(MAXB, dtype=jnp.int32) < used
        blocks = jnp.where(live_slots[:, None, None], blocks, jnp.zeros((), blocks.dtype))
        stacked = blocks.astype(jnp.float32).reshape(-1, blocks.shape[2])
        gram_full = jnp.dot(stacked.T, stacked, precision=highest) / (2.0 * K)
        gram_matrix = lax.optimization_barrier(gram_full.astype(jnp.bfloat16)).astype(jnp.float32)
        members = ensemble[:, region, patch, :].astype(jnp.float32)
        first_term = jnp.dot(gram_matrix, members, precision=highest).astype(jnp.bfloat16)
        first_term = lax.optimization_barrier(first_term).astype(jnp.float32)
        second_term = jnp.dot(gram_matrix, first_term, precision=highest)
        return (members - first_term + second_term).astype(jnp.bfloat16)

    result = lax.map(one_patch, jnp.arange(regions * patches, dtype=jnp.int32))
    result = result.reshape(regions, patches, result.shape[1], result.shape[2])
    return jnp.transpose(result, (2, 0, 1, 3))
```

```python
import functools

import jax
import jax.numpy as jnp
from jax import lax
from jax.experimental import pallas as pl
from jax.experimental.pallas import tpu as pltpu
from jax.sharding import PartitionSpec as P

K = 1024
OBS_DEV = 5
MAXB = 3
CHUNKS = 2
MESH = pl.DeviceIdType.MESH


def kernel(
    nz, nx, nr,
    ids_ref, src_ref, count_ref, ens_hbm, obs_hbm, out_ref,
    ens, packed, xbuf, obuf, rbuf, obs, gram, first,
    ens_sem, obs_sem, obs_send, obs_recv, in_send, in_recv, out_send, out_recv,
):
    me = lax.axis_index("member")
    region = lax.axis_index("region")
    n = nz * nx
    z, x = me // nx, me % nx
    chunks, width = packed.shape[0], packed.shape[3]
    rows = packed.shape[2]
    groups = n // 16

    def peer(i):
        step = i // nx
        dz = nz // 2 + ((step + 1) // 2) * (1 - 2 * (step % 2))
        dx = i % nx + 1
        return ((z + dz + nz) % nz) * nx + (x + dx) % nx

    above, below = (region + 1) % nr, (region + nr - 1) % nr
    barrier = pltpu.get_barrier_semaphore()

    def greet(i, carry):
        pl.semaphore_signal(barrier, inc=1, device_id={"member": peer(i)}, device_id_type=MESH)
        return carry

    lax.fori_loop(0, n - 1, greet, 0)
    for other in (above, below):
        pl.semaphore_signal(barrier, inc=1, device_id={"region": other}, device_id_type=MESH)

    loads = []
    for c in range(chunks):
        cols = pl.ds(c * width, width)
        load = pltpu.make_async_copy(ens_hbm.at[:, 0, :, cols], ens.at[:, :, cols], ens_sem.at[c])
        load.start()
        loads.append(load)
    own_obs = pltpu.make_async_copy(obs_hbm.at[0, 0], obs.at[1], obs_sem)
    own_obs.start()

    i0 = lax.broadcasted_iota(jnp.int32, (256, 256), 0)
    i1 = lax.broadcasted_iota(jnp.int32, (256, 256), 1)
    swap = ((i0 % 16) * 16 + i0 // 16 == i1).astype(jnp.bfloat16)

    def exchange(c):
        return jnp.dot(swap, c, preferred_element_type=jnp.float32).astype(jnp.bfloat16)

    def pack(c):
        for g in range(groups):
            part = ens[:, 16 * g : 16 * g + 16, c * width : (c + 1) * width]
            packed[c, 16 * g : 16 * g + 16] = exchange(part.reshape(256, width)).reshape(16, 16, width)

    def send(c, source, target, send_sem, recv_sem):
        def one(i, carry):
            other = peer(i)
            pltpu.make_async_remote_copy(
                src_ref=source.at[c, other],
                dst_ref=target.at[c, me],
                send_sem=send_sem.at[c],
                recv_sem=recv_sem.at[c],
                device_id={"member": other},
                device_id_type=MESH,
            ).start()
            return carry

        lax.fori_loop(0, n - 1, one, 0)
        target[c, me] = source[c, me]

    def whole(c, source, target, send_sem, recv_sem):
        part = pl.ds(0, n - 1)
        return pltpu.make_async_remote_copy(
            src_ref=source.at[c, part],
            dst_ref=target.at[c, part],
            send_sem=send_sem.at[c],
            recv_sem=recv_sem.at[c],
            device_id={"member": peer(0)},
            device_id_type=MESH,
        )

    incoming = (packed, xbuf, in_send, in_recv)
    outgoing = (obuf, rbuf, out_send, out_recv)

    loads[0].wait()
    pack(0)
    pl.semaphore_wait(barrier, n + 1)
    obs_copies = []
    for slot, other in ((0, above), (2, below)):
        copy = pltpu.make_async_remote_copy(
            src_ref=obs_hbm.at[0, 0],
            dst_ref=obs.at[slot],
            send_sem=obs_send.at[slot // 2],
            recv_sem=obs_recv.at[slot // 2],
            device_id={"region": other},
            device_id_type=MESH,
        )
        copy.start()
        obs_copies.append(copy)
    send(0, *incoming)
    for c in range(1, chunks):
        loads[c].wait()
        pack(c)
        send(c, *incoming)

    own_obs.wait()
    for copy in obs_copies:
        copy.wait()
    blocks = []
    for j in range(MAXB):
        block = obs[src_ref[j], ids_ref[j]]
        blocks.append(jnp.where(j < count_ref[0], block, jnp.zeros((), block.dtype)))
    stacked = jnp.concatenate(blocks, axis=0)
    tile = 256
    for t in range(K // tile):
        full = lax.dot_general(
            stacked[:, t * tile : (t + 1) * tile], stacked, (((0,), (0,)), ((), ())),
            preferred_element_type=jnp.float32,
        )
        gram[t * tile : (t + 1) * tile, :] = (full / (2.0 * K)).astype(jnp.bfloat16)

    for c in range(chunks):
        whole(c, *incoming).wait_recv()

        @pl.loop(0, K // tile)
        def _(t):
            members = xbuf[c].reshape(K, width)
            part = pl.ds(t * tile, tile)
            first[part, :] = jnp.dot(
                gram[part, :], members, preferred_element_type=jnp.float32
            ).astype(jnp.bfloat16)

        @pl.loop(0, K // tile)
        def _(t):
            part = pl.ds(t * tile, tile)
            lots = pl.ds(t * (tile // rows), tile // rows)
            second = jnp.dot(gram[part, :], first[...], preferred_element_type=jnp.float32)
            members = xbuf[c, lots].reshape(tile, width).astype(jnp.float32)
            fresh = members - first[part, :].astype(jnp.float32) + second
            obuf[c, lots] = fresh.astype(jnp.bfloat16).reshape(tile // rows, rows, width)

        send(c, *outgoing)

    for c in range(chunks):
        whole(c, *outgoing).wait_recv()
        for g in range(groups):
            part = rbuf[c, 16 * g : 16 * g + 16].reshape(256, width)
            out_ref[:, 0, 16 * g : 16 * g + 16, c * width : (c + 1) * width] = exchange(part).reshape(16, 16, width)
    for c in range(chunks):
        whole(c, *incoming).wait_send()
        whole(c, *outgoing).wait_send()


def solution(mesh):
    nr = mesh.shape["region"]
    n = mesh.shape["member"]
    nx = 4
    nz = n // nx

    def shards(ensemble, obs_store, block_ids, block_src, block_count):
        rows, _, patches, values = ensemble.shape
        width = values // CHUNKS
        piece = pltpu.VMEM((CHUNKS, n, rows, width), jnp.bfloat16)
        dma = pltpu.SemaphoreType.DMA
        return pl.pallas_call(
            functools.partial(kernel, nz, nx, nr),
            out_shape=jax.ShapeDtypeStruct(ensemble.shape, jnp.bfloat16),
            in_specs=[pl.BlockSpec(memory_space=pltpu.SMEM)] * 3
            + [pl.BlockSpec(memory_space=pl.ANY)] * 2,
            out_specs=pl.BlockSpec(memory_space=pltpu.VMEM),
            scratch_shapes=[
                pltpu.VMEM((rows, patches, values), jnp.bfloat16),
                piece, piece, piece, piece,
                pltpu.VMEM((3,) + obs_store.shape[2:], jnp.bfloat16),
                pltpu.VMEM((K, K), jnp.bfloat16),
                pltpu.VMEM((K, width), jnp.bfloat16),
                dma((CHUNKS,)), dma, dma((2,)), dma((2,)),
                dma((CHUNKS,)), dma((CHUNKS,)), dma((CHUNKS,)), dma((CHUNKS,)),
            ],
            compiler_params=pltpu.CompilerParams(
                collective_id=0, has_side_effects=True, vmem_limit_bytes=62 << 20
            ),
            name="analysis",
        )(
            block_ids.reshape(MAXB), block_src.reshape(MAXB), block_count.reshape(1),
            ensemble, obs_store,
        )

    return jax.shard_map(
        shards,
        mesh=mesh,
        in_specs=(
            P("member", "region", None, None),
            P("region", "member", None, None, None),
            P("region", "member", None),
            P("region", "member", None),
            P("region", "member"),
        ),
        out_specs=P("member", "region", None, None),
        check_vma=False,
    )
```

```python
import functools

import jax
import jax.numpy as jnp
from jax import lax
from jax.experimental import pallas as pl
from jax.experimental.pallas import tpu as pltpu
from jax.sharding import PartitionSpec as P

K = 1024
OBS_DEV = 5
MAXB = 3
CHUNKS = 2
MESH = pl.DeviceIdType.MESH


def kernel(
    nz, nx, nr,
    ids_hbm, src_hbm, ens_hbm, obs_hbm, count_ref, out_ref,
    ids_ref, src_ref, ens, packed, xbuf, obuf, rbuf, obs, gram, first,
    ens_sem, obs_sem, obs_send, obs_recv, in_send, in_recv, out_send, out_recv, int_sem,
):
    me = lax.axis_index("member")
    region = lax.axis_index("region")
    n = nz * nx
    z, x = me // nx, me % nx
    chunks, width = packed.shape[0], packed.shape[3]
    rows = packed.shape[2]
    groups = n // 16

    def peer(i):
        step = i // nx
        dz = nz // 2 + ((step + 1) // 2) * (1 - 2 * (step % 2))
        dx = i % nx + 1
        return ((z + dz + nz) % nz) * nx + (x + dx) % nx

    above, below = (region + 1) % nr, (region + nr - 1) % nr
    barrier = pltpu.get_barrier_semaphore()

    def greet(i, carry):
        pl.semaphore_signal(barrier, inc=1, device_id={"member": peer(i)}, device_id_type=MESH)
        return carry

    lax.fori_loop(0, n - 1, greet, 0)
    for other in (above, below):
        pl.semaphore_signal(barrier, inc=1, device_id={"region": other}, device_id_type=MESH)

    loads = []
    for c in range(chunks):
        cols = pl.ds(c * width, width)
        load = pltpu.make_async_copy(ens_hbm.at[:, 0, :, cols], ens.at[:, :, cols], ens_sem.at[c])
        load.start()
        loads.append(load)
    own_obs = pltpu.make_async_copy(obs_hbm.at[0, 0], obs.at[1], obs_sem)
    own_obs.start()
    ints = []
    for i, (source, target) in enumerate(((ids_hbm, ids_ref), (src_hbm, src_ref))):
        load = pltpu.make_async_copy(source, target, int_sem.at[i])
        load.start()
        ints.append(load)

    i0 = lax.broadcasted_iota(jnp.int32, (256, 256), 0)
    i1 = lax.broadcasted_iota(jnp.int32, (256, 256), 1)
    swap = ((i0 % 16) * 16 + i0 // 16 == i1).astype(jnp.bfloat16)

    def exchange(c):
        return jnp.dot(swap, c, preferred_element_type=jnp.float32).astype(jnp.bfloat16)

    def pack(c):
        for g in range(groups):
            part = ens[:, 16 * g : 16 * g + 16, c * width : (c + 1) * width]
            packed[c, 16 * g : 16 * g + 16] = exchange(part.reshape(256, width)).reshape(16, 16, width)

    def send(c, source, target, send_sem, recv_sem):
        def one(i, carry):
            other = peer(i)
            pltpu.make_async_remote_copy(
                src_ref=source.at[c, other],
                dst_ref=target.at[c, me],
                send_sem=send_sem.at[c],
                recv_sem=recv_sem.at[c],
                device_id={"member": other},
                device_id_type=MESH,
            ).start()
            return carry

        lax.fori_loop(0, n - 1, one, 0)
        target[c, me] = source[c, me]

    def whole(c, source, target, send_sem, recv_sem):
        part = pl.ds(0, n - 1)
        return pltpu.make_async_remote_copy(
            src_ref=source.at[c, part],
            dst_ref=target.at[c, part],
            send_sem=send_sem.at[c],
            recv_sem=recv_sem.at[c],
            device_id={"member": peer(0)},
            device_id_type=MESH,
        )

    incoming = (packed, xbuf, in_send, in_recv)
    outgoing = (obuf, rbuf, out_send, out_recv)

    loads[0].wait()
    pack(0)
    pl.semaphore_wait(barrier, n + 1)
    obs_copies = []
    for slot, other in ((0, above), (2, below)):
        copy = pltpu.make_async_remote_copy(
            src_ref=obs_hbm.at[0, 0],
            dst_ref=obs.at[slot],
            send_sem=obs_send.at[slot // 2],
            recv_sem=obs_recv.at[slot // 2],
            device_id={"region": other},
            device_id_type=MESH,
        )
        copy.start()
        obs_copies.append(copy)
    send(0, *incoming)
    for c in range(1, chunks):
        loads[c].wait()
        pack(c)
        send(c, *incoming)

    for load in ints:
        load.wait()
    own_obs.wait()
    for copy in obs_copies:
        copy.wait()
    blocks = []
    for j in range(MAXB):
        block = obs[src_ref[0, 0, j], ids_ref[0, 0, j]]
        blocks.append(jnp.where(j < count_ref[0, 0], block, jnp.zeros((), block.dtype)))
    stacked = jnp.concatenate(blocks, axis=0)
    tile = 256
    for t in range(K // tile):
        full = lax.dot_general(
            stacked[:, t * tile : (t + 1) * tile], stacked, (((0,), (0,)), ((), ())),
            preferred_element_type=jnp.float32,
        )
        gram[t * tile : (t + 1) * tile, :] = (full / (2.0 * K)).astype(jnp.bfloat16)

    for c in range(chunks):
        whole(c, *incoming).wait_recv()

        @pl.loop(0, K // tile)
        def _(t):
            members = xbuf[c].reshape(K, width)
            part = pl.ds(t * tile, tile)
            first[part, :] = jnp.dot(
                gram[part, :], members, preferred_element_type=jnp.float32
            ).astype(jnp.bfloat16)

        @pl.loop(0, K // tile)
        def _(t):
            part = pl.ds(t * tile, tile)
            lots = pl.ds(t * (tile // rows), tile // rows)
            second = jnp.dot(gram[part, :], first[...], preferred_element_type=jnp.float32)
            members = xbuf[c, lots].reshape(tile, width).astype(jnp.float32)
            fresh = members - first[part, :].astype(jnp.float32) + second
            obuf[c, lots] = fresh.astype(jnp.bfloat16).reshape(tile // rows, rows, width)

        send(c, *outgoing)

    for c in range(chunks):
        whole(c, *outgoing).wait_recv()
        for g in range(groups):
            part = rbuf[c, 16 * g : 16 * g + 16].reshape(256, width)
            out_ref[:, 0, 16 * g : 16 * g + 16, c * width : (c + 1) * width] = exchange(part).reshape(16, 16, width)
    for c in range(chunks):
        whole(c, *incoming).wait_send()
        whole(c, *outgoing).wait_send()


def solution(mesh):
    nr = mesh.shape["region"]
    n = mesh.shape["member"]
    nx = 4
    nz = n // nx

    def shards(ensemble, obs_store, block_ids, block_src, block_count):
        rows, _, patches, values = ensemble.shape
        width = values // CHUNKS
        piece = pltpu.VMEM((CHUNKS, n, rows, width), jnp.bfloat16)
        dma = pltpu.SemaphoreType.DMA
        return pl.pallas_call(
            functools.partial(kernel, nz, nx, nr),
            out_shape=jax.ShapeDtypeStruct(ensemble.shape, jnp.bfloat16),
            in_specs=[pl.BlockSpec(memory_space=pltpu.HBM)] * 4
            + [pl.BlockSpec(memory_space=pltpu.SMEM)],
            out_specs=pl.BlockSpec(memory_space=pltpu.VMEM),
            scratch_shapes=[
                pltpu.SMEM((1, 1, MAXB), jnp.int32),
                pltpu.SMEM((1, 1, MAXB), jnp.int32),
                pltpu.VMEM((rows, patches, values), jnp.bfloat16),
                piece, piece, piece, piece,
                pltpu.VMEM((3,) + obs_store.shape[2:], jnp.bfloat16),
                pltpu.VMEM((K, K), jnp.bfloat16),
                pltpu.VMEM((K, width), jnp.bfloat16),
                dma((CHUNKS,)), dma, dma((2,)), dma((2,)),
                dma((CHUNKS,)), dma((CHUNKS,)), dma((CHUNKS,)), dma((CHUNKS,)), dma((2,)),
            ],
            compiler_params=pltpu.CompilerParams(
                collective_id=0, has_side_effects=True, vmem_limit_bytes=40 << 20
            ),
            name="analysis",
        )(
            *(
                pltpu.with_memory_space_constraint(value, pltpu.HBM)
                for value in (block_ids, block_src, ensemble, obs_store)
            ),
            block_count,
        )

    return jax.shard_map(
        shards,
        mesh=mesh,
        in_specs=(
            P("member", "region", None, None),
            P("region", "member", None, None, None),
            P("region", "member", None),
            P("region", "member", None),
            P("region", "member"),
        ),
        out_specs=P("member", "region", None, None),
        check_vma=False,
    )
```

```python
import functools

import jax
import jax.numpy as jnp
from jax import lax
from jax.experimental import pallas as pl
from jax.experimental.pallas import tpu as pltpu
from jax.sharding import PartitionSpec as P

K = 1024
OBS_DEV = 5
MAXB = 3
CHUNKS = 2
MESH = pl.DeviceIdType.MESH


def kernel(
    nz, nx, nr,
    ids_hbm, src_hbm, ens_hbm, obs_hbm, count_ref, out_ref,
    ids_ref, src_ref, ens, packed, xbuf, obuf, rbuf, obs, gram, first,
    ens_sem, obs_sem, obs_send, obs_recv, in_send, in_recv, out_send, out_recv, int_sem,
    chain, arrived,
):
    me = lax.axis_index("member")
    region = lax.axis_index("region")
    n = nz * nx
    z, x = me // nx, me % nx
    chunks, width = packed.shape[0], packed.shape[3]
    rows = packed.shape[2]
    groups = n // 16

    above, below = (region + 1) % nr, (region + nr - 1) % nr
    barrier = pltpu.get_barrier_semaphore()

    def greet(device):
        pl.semaphore_signal(barrier, inc=1, device_id=device, device_id_type=MESH)

    for dx in range(1, nx):
        greet({"member": z * nx + (x + dx) % nx})

    @pl.when(z > 0)
    def _():
        greet({"member": me - nx})

    @pl.when(z < nz - 1)
    def _():
        greet({"member": me + nx})

    for other in (above, below):
        greet({"region": other})

    loads = []
    for c in range(chunks):
        cols = pl.ds(c * width, width)
        load = pltpu.make_async_copy(ens_hbm.at[:, 0, :, cols], ens.at[:, :, cols], ens_sem.at[c])
        load.start()
        loads.append(load)
    own_obs = pltpu.make_async_copy(obs_hbm.at[0, 0], obs.at[1], obs_sem)
    own_obs.start()
    ints = []
    for i, (source, target) in enumerate(((ids_hbm, ids_ref), (src_hbm, src_ref))):
        load = pltpu.make_async_copy(source, target, int_sem.at[i])
        load.start()
        ints.append(load)

    i0 = lax.broadcasted_iota(jnp.int32, (256, 256), 0)
    i1 = lax.broadcasted_iota(jnp.int32, (256, 256), 1)
    swap = ((i0 % 16) * 16 + i0 // 16 == i1).astype(jnp.bfloat16)

    def exchange(c):
        return jnp.dot(swap, c, preferred_element_type=jnp.float32).astype(jnp.bfloat16)

    def pack(c):
        for g in range(groups):
            part = ens[:, 16 * g : 16 * g + 16, c * width : (c + 1) * width]
            packed[c, 16 * g : 16 * g + 16] = exchange(part.reshape(256, width)).reshape(16, 16, width)

    def send_row(c, row, source, target, send_sem, recv_sem):
        for dx in range(nx):
            other = row * nx + (x + dx) % nx

            def start(other=other):
                pltpu.make_async_remote_copy(
                    src_ref=source.at[c, other],
                    dst_ref=target.at[c, me],
                    send_sem=send_sem.at[c],
                    recv_sem=recv_sem.at[c],
                    device_id={"member": other},
                    device_id_type=MESH,
                ).start()

            if dx == 0:
                pl.when(row != z)(start)
            else:
                start()

    def far_first(chosen, c, source, target, send_sem, recv_sem):
        def one(step, carry):
            dz = nz // 2 + ((step + 1) // 2) * (1 - 2 * (step % 2))
            row = (z + dz + nz) % nz
            pl.when(chosen(row))(lambda: send_row(c, row, source, target, send_sem, recv_sem))
            return carry

        lax.fori_loop(0, nz, one, 0)

    def whole(c, source, target, send_sem, recv_sem):
        part = pl.ds(0, n - 1)
        return pltpu.make_async_remote_copy(
            src_ref=source.at[c, part],
            dst_ref=target.at[c, part],
            send_sem=send_sem.at[c],
            recv_sem=recv_sem.at[c],
            device_id={"member": (me + 1) % n},
            device_id_type=MESH,
        )

    incoming = (packed, xbuf, in_send, in_recv)
    outgoing = (obuf, rbuf, out_send, out_recv)

    for c in range(chunks):
        loads[c].wait()
        pack(c)
        xbuf[c, me] = packed[c, me]
    inner = jnp.where(z > 0, 1, 0) + jnp.where(z < nz - 1, 1, 0)
    pl.semaphore_wait(barrier, nx + 1 + inner)

    @pl.when(z > 0)
    def _():
        pl.semaphore_wait(chain, 1)

    @pl.when(z < nz - 1)
    def _():
        pl.semaphore_signal(chain, inc=1, device_id={"member": me + nx}, device_id_type=MESH)

    def arrive(i, carry):
        pl.semaphore_signal(arrived.at[z], inc=1, device_id={"member": i}, device_id_type=MESH)
        return carry

    lax.fori_loop(0, z * nx, arrive, 0)

    obs_copies = []
    for slot, other in ((0, above), (2, below)):
        copy = pltpu.make_async_remote_copy(
            src_ref=obs_hbm.at[0, 0],
            dst_ref=obs.at[slot],
            send_sem=obs_send.at[slot // 2],
            recv_sem=obs_recv.at[slot // 2],
            device_id={"region": other},
            device_id_type=MESH,
        )
        copy.start()
        obs_copies.append(copy)
    far_first(lambda row: row <= z, 0, *incoming)

    def fresh_row(row, carry):
        pl.semaphore_wait(arrived.at[row], nx)
        send_row(0, row, *incoming)
        return carry

    lax.fori_loop(z + 1, nz, fresh_row, 0)
    for c in range(1, chunks):
        far_first(lambda row: row >= 0, c, *incoming)

    for load in ints:
        load.wait()
    own_obs.wait()
    for copy in obs_copies:
        copy.wait()
    blocks = []
    for j in range(MAXB):
        block = obs[src_ref[0, 0, j], ids_ref[0, 0, j]]
        blocks.append(jnp.where(j < count_ref[0, 0], block, jnp.zeros((), block.dtype)))
    stacked = jnp.concatenate(blocks, axis=0)
    tile = 256
    for t in range(K // tile):
        full = lax.dot_general(
            stacked[:, t * tile : (t + 1) * tile], stacked, (((0,), (0,)), ((), ())),
            preferred_element_type=jnp.float32,
        )
        gram[t * tile : (t + 1) * tile, :] = (full / (2.0 * K)).astype(jnp.bfloat16)

    for c in range(chunks):
        whole(c, *incoming).wait_recv()

        @pl.loop(0, K // tile)
        def _(t):
            members = xbuf[c].reshape(K, width)
            part = pl.ds(t * tile, tile)
            first[part, :] = jnp.dot(
                gram[part, :], members, preferred_element_type=jnp.float32
            ).astype(jnp.bfloat16)

        @pl.loop(0, K // tile)
        def _(t):
            part = pl.ds(t * tile, tile)
            lots = pl.ds(t * (tile // rows), tile // rows)
            second = jnp.dot(gram[part, :], first[...], preferred_element_type=jnp.float32)
            members = xbuf[c, lots].reshape(tile, width).astype(jnp.float32)
            fresh = members - first[part, :].astype(jnp.float32) + second
            obuf[c, lots] = fresh.astype(jnp.bfloat16).reshape(tile // rows, rows, width)

        rbuf[c, me] = obuf[c, me]
        if c < chunks - 1:
            far_first(lambda row: row >= 0, c, *outgoing)
        else:
            half = nz // 2
            far_first(lambda row: (row < half) | (z < half), c, *outgoing)
            far_first(lambda row: (row >= half) & (z >= half), c, *outgoing)

    for c in range(chunks):
        whole(c, *outgoing).wait_recv()
        for g in range(groups):
            part = rbuf[c, 16 * g : 16 * g + 16].reshape(256, width)
            out_ref[:, 0, 16 * g : 16 * g + 16, c * width : (c + 1) * width] = exchange(part).reshape(16, 16, width)
    for c in range(chunks):
        whole(c, *incoming).wait_send()
        whole(c, *outgoing).wait_send()


def solution(mesh):
    nr = mesh.shape["region"]
    n = mesh.shape["member"]
    nx = 4
    nz = n // nx

    def shards(ensemble, obs_store, block_ids, block_src, block_count):
        rows, _, patches, values = ensemble.shape
        width = values // CHUNKS
        piece = pltpu.VMEM((CHUNKS, n, rows, width), jnp.bfloat16)
        dma = pltpu.SemaphoreType.DMA
        return pl.pallas_call(
            functools.partial(kernel, nz, nx, nr),
            out_shape=jax.ShapeDtypeStruct(ensemble.shape, jnp.bfloat16),
            in_specs=[pl.BlockSpec(memory_space=pltpu.HBM)] * 4
            + [pl.BlockSpec(memory_space=pltpu.SMEM)],
            out_specs=pl.BlockSpec(memory_space=pltpu.VMEM),
            scratch_shapes=[
                pltpu.SMEM((1, 1, MAXB), jnp.int32),
                pltpu.SMEM((1, 1, MAXB), jnp.int32),
                pltpu.VMEM((rows, patches, values), jnp.bfloat16),
                piece, piece, piece, piece,
                pltpu.VMEM((3,) + obs_store.shape[2:], jnp.bfloat16),
                pltpu.VMEM((K, K), jnp.bfloat16),
                pltpu.VMEM((K, width), jnp.bfloat16),
                dma((CHUNKS,)), dma, dma((2,)), dma((2,)),
                dma((CHUNKS,)), dma((CHUNKS,)), dma((CHUNKS,)), dma((CHUNKS,)), dma((2,)),
                pltpu.SemaphoreType.REGULAR, pltpu.SemaphoreType.REGULAR((nz,)),
            ],
            compiler_params=pltpu.CompilerParams(
                collective_id=0, has_side_effects=True, vmem_limit_bytes=40 << 20
            ),
            name="analysis",
        )(
            *(
                pltpu.with_memory_space_constraint(value, pltpu.HBM)
                for value in (block_ids, block_src, ensemble, obs_store)
            ),
            block_count,
        )

    return jax.shard_map(
        shards,
        mesh=mesh,
        in_specs=(
            P("member", "region", None, None),
            P("region", "member", None, None, None),
            P("region", "member", None),
            P("region", "member", None),
            P("region", "member"),
        ),
        out_specs=P("member", "region", None, None),
        check_vma=False,
    )
```

```python
import functools

import jax
import jax.numpy as jnp
from jax import lax
from jax.experimental import pallas as pl
from jax.experimental.pallas import tpu as pltpu
from jax.sharding import PartitionSpec as P

K = 1024
OBS_DEV = 5
MAXB = 3
CHUNKS = 2
MESH = pl.DeviceIdType.MESH


def kernel(
    nz, nx, nr,
    ids_hbm, src_hbm, ens_hbm, obs_hbm, count_ref, out_ref,
    ids_ref, src_ref, ens, packed, xbuf, obuf, rbuf, obs, gram, first,
    ens_sem, obs_sem, obs_send, obs_recv, in_send, in_recv, out_send, out_recv, int_sem,
    chain, arrived,
):
    me = lax.axis_index("member")
    region = lax.axis_index("region")
    n = nz * nx
    z, x = me // nx, me % nx
    chunks, width = packed.shape[0], packed.shape[3]
    rows = packed.shape[2]
    groups = n // 16

    above, below = (region + 1) % nr, (region + nr - 1) % nr
    late = 11
    special = (region <= 1) | (region == nr - 1)

    def place(row):
        return jnp.where(special, jnp.where(row == 0, late, jnp.where(row <= late, row - 1, row)), row)

    def row_at(pos):
        return jnp.where(special, jnp.where(pos == late, 0, jnp.where(pos < late, pos + 1, pos)), pos)

    pos = place(z)
    ahead, behind = row_at(pos + 1) * nx + x, row_at(pos - 1) * nx + x
    barrier = pltpu.get_barrier_semaphore()

    def greet(device):
        pl.semaphore_signal(barrier, inc=1, device_id=device, device_id_type=MESH)

    for dx in range(1, nx):
        greet({"member": z * nx + (x + dx) % nx})

    @pl.when(pos > 0)
    def _():
        greet({"member": behind})

    @pl.when(pos < nz - 1)
    def _():
        greet({"member": ahead})

    for other in (above, below):
        greet({"region": other})

    loads = []
    for c in range(chunks):
        cols = pl.ds(c * width, width)
        load = pltpu.make_async_copy(ens_hbm.at[:, 0, :, cols], ens.at[:, :, cols], ens_sem.at[c])
        load.start()
        loads.append(load)
    own_obs = pltpu.make_async_copy(obs_hbm.at[0, 0], obs.at[1], obs_sem)
    own_obs.start()
    ints = []
    for i, (source, target) in enumerate(((ids_hbm, ids_ref), (src_hbm, src_ref))):
        load = pltpu.make_async_copy(source, target, int_sem.at[i])
        load.start()
        ints.append(load)

    i0 = lax.broadcasted_iota(jnp.int32, (256, 256), 0)
    i1 = lax.broadcasted_iota(jnp.int32, (256, 256), 1)
    swap = ((i0 % 16) * 16 + i0 // 16 == i1).astype(jnp.bfloat16)

    def exchange(c):
        return jnp.dot(swap, c, preferred_element_type=jnp.float32).astype(jnp.bfloat16)

    def pack(c):
        for g in range(groups):
            part = ens[:, 16 * g : 16 * g + 16, c * width : (c + 1) * width]
            packed[c, 16 * g : 16 * g + 16] = exchange(part.reshape(256, width)).reshape(16, 16, width)

    def send_row(c, row, source, target, send_sem, recv_sem):
        for dx in range(nx):
            other = row * nx + (x + dx) % nx

            def start(other=other):
                pltpu.make_async_remote_copy(
                    src_ref=source.at[c, other],
                    dst_ref=target.at[c, me],
                    send_sem=send_sem.at[c],
                    recv_sem=recv_sem.at[c],
                    device_id={"member": other},
                    device_id_type=MESH,
                ).start()

            if dx == 0:
                pl.when(row != z)(start)
            else:
                start()

    def far_first(chosen, c, source, target, send_sem, recv_sem):
        def one(step, carry):
            dz = nz // 2 + ((step + 1) // 2) * (1 - 2 * (step % 2))
            row = (z + dz + nz) % nz
            pl.when(chosen(row))(lambda: send_row(c, row, source, target, send_sem, recv_sem))
            return carry

        lax.fori_loop(0, nz, one, 0)

    def whole(c, source, target, send_sem, recv_sem):
        part = pl.ds(0, n - 1)
        return pltpu.make_async_remote_copy(
            src_ref=source.at[c, part],
            dst_ref=target.at[c, part],
            send_sem=send_sem.at[c],
            recv_sem=recv_sem.at[c],
            device_id={"member": (me + 1) % n},
            device_id_type=MESH,
        )

    incoming = (packed, xbuf, in_send, in_recv)
    outgoing = (obuf, rbuf, out_send, out_recv)

    for c in range(chunks):
        loads[c].wait()
        pack(c)
        xbuf[c, me] = packed[c, me]
    inner = jnp.where(pos > 0, 1, 0) + jnp.where(pos < nz - 1, 1, 0)
    pl.semaphore_wait(barrier, nx + 1 + inner)

    @pl.when(pos > 0)
    def _():
        pl.semaphore_wait(chain, 1)

    @pl.when(pos < nz - 1)
    def _():
        pl.semaphore_signal(chain, inc=1, device_id={"member": ahead}, device_id_type=MESH)

    def arrive(i, carry):
        pl.semaphore_signal(arrived.at[z], inc=1, device_id={"member": row_at(i // nx) * nx + i % nx}, device_id_type=MESH)
        return carry

    lax.fori_loop(0, pos * nx, arrive, 0)

    obs_copies = []
    for slot, other in ((0, above), (2, below)):
        copy = pltpu.make_async_remote_copy(
            src_ref=obs_hbm.at[0, 0],
            dst_ref=obs.at[slot],
            send_sem=obs_send.at[slot // 2],
            recv_sem=obs_recv.at[slot // 2],
            device_id={"region": other},
            device_id_type=MESH,
        )
        copy.start()
        obs_copies.append(copy)
    far_first(lambda row: place(row) <= pos, 0, *incoming)

    def fresh_row(p, carry):
        row = row_at(p)
        pl.semaphore_wait(arrived.at[row], nx)
        send_row(0, row, *incoming)
        return carry

    lax.fori_loop(pos + 1, nz, fresh_row, 0)
    for c in range(1, chunks):
        far_first(lambda row: row >= 0, c, *incoming)

    for load in ints:
        load.wait()
    own_obs.wait()
    for copy in obs_copies:
        copy.wait()
    blocks = []
    for j in range(MAXB):
        block = obs[src_ref[0, 0, j], ids_ref[0, 0, j]]
        blocks.append(jnp.where(j < count_ref[0, 0], block, jnp.zeros((), block.dtype)))
    stacked = jnp.concatenate(blocks, axis=0)
    tile = 256
    for t in range(K // tile):
        full = lax.dot_general(
            stacked[:, t * tile : (t + 1) * tile], stacked, (((0,), (0,)), ((), ())),
            preferred_element_type=jnp.float32,
        )
        gram[t * tile : (t + 1) * tile, :] = (full / (2.0 * K)).astype(jnp.bfloat16)

    for c in range(chunks):
        whole(c, *incoming).wait_recv()

        @pl.loop(0, K // tile)
        def _(t):
            members = xbuf[c].reshape(K, width)
            part = pl.ds(t * tile, tile)
            first[part, :] = jnp.dot(
                gram[part, :], members, preferred_element_type=jnp.float32
            ).astype(jnp.bfloat16)

        @pl.loop(0, K // tile)
        def _(t):
            part = pl.ds(t * tile, tile)
            lots = pl.ds(t * (tile // rows), tile // rows)
            second = jnp.dot(gram[part, :], first[...], preferred_element_type=jnp.float32)
            members = xbuf[c, lots].reshape(tile, width).astype(jnp.float32)
            fresh = members - first[part, :].astype(jnp.float32) + second
            obuf[c, lots] = fresh.astype(jnp.bfloat16).reshape(tile // rows, rows, width)

        rbuf[c, me] = obuf[c, me]
        if c < chunks - 1:
            far_first(lambda row: row >= 0, c, *outgoing)
        else:
            half = nz // 2
            far_first(lambda row: (row < half) | (z < half), c, *outgoing)
            far_first(lambda row: (row >= half) & (z >= half), c, *outgoing)

    for c in range(chunks):
        whole(c, *outgoing).wait_recv()
        for g in range(groups):
            part = rbuf[c, 16 * g : 16 * g + 16].reshape(256, width)
            out_ref[:, 0, 16 * g : 16 * g + 16, c * width : (c + 1) * width] = exchange(part).reshape(16, 16, width)
    for c in range(chunks):
        whole(c, *incoming).wait_send()
        whole(c, *outgoing).wait_send()


def solution(mesh):
    nr = mesh.shape["region"]
    n = mesh.shape["member"]
    nx = 4
    nz = n // nx

    def shards(ensemble, obs_store, block_ids, block_src, block_count):
        rows, _, patches, values = ensemble.shape
        width = values // CHUNKS
        piece = pltpu.VMEM((CHUNKS, n, rows, width), jnp.bfloat16)
        dma = pltpu.SemaphoreType.DMA
        return pl.pallas_call(
            functools.partial(kernel, nz, nx, nr),
            out_shape=jax.ShapeDtypeStruct(ensemble.shape, jnp.bfloat16),
            in_specs=[pl.BlockSpec(memory_space=pltpu.HBM)] * 4
            + [pl.BlockSpec(memory_space=pltpu.SMEM)],
            out_specs=pl.BlockSpec(memory_space=pltpu.VMEM),
            scratch_shapes=[
                pltpu.SMEM((1, 1, MAXB), jnp.int32),
                pltpu.SMEM((1, 1, MAXB), jnp.int32),
                pltpu.VMEM((rows, patches, values), jnp.bfloat16),
                piece, piece, piece, piece,
                pltpu.VMEM((3,) + obs_store.shape[2:], jnp.bfloat16),
                pltpu.VMEM((K, K), jnp.bfloat16),
                pltpu.VMEM((K, width), jnp.bfloat16),
                dma((CHUNKS,)), dma, dma((2,)), dma((2,)),
                dma((CHUNKS,)), dma((CHUNKS,)), dma((CHUNKS,)), dma((CHUNKS,)), dma((2,)),
                pltpu.SemaphoreType.REGULAR, pltpu.SemaphoreType.REGULAR((nz,)),
            ],
            compiler_params=pltpu.CompilerParams(
                collective_id=0, has_side_effects=True, vmem_limit_bytes=40 << 20
            ),
            name="analysis",
        )(
            *(
                pltpu.with_memory_space_constraint(value, pltpu.HBM)
                for value in (block_ids, block_src, ensemble, obs_store)
            ),
            block_count,
        )

    return jax.shard_map(
        shards,
        mesh=mesh,
        in_specs=(
            P("member", "region", None, None),
            P("region", "member", None, None, None),
            P("region", "member", None),
            P("region", "member", None),
            P("region", "member"),
        ),
        out_specs=P("member", "region", None, None),
        check_vma=False,
    )
```
